256 devices in a mesh: pix: 16 (over x_hi, z), peak: 16 (over y, x_lo, core).
Axes of the slice: x: 4 (x_hi: 2, x_lo: 2; x = x_hi * 2 + x_lo), y: 4, z: 8, core: 2. Of those that a mesh axis runs over, the one named last changes fastest.
Arguments:
- cube: bfloat16 [65536, 8, 2048], P('pix', None, 'peak'), may hold values from -6 to 6
- pix_factor: bfloat16 [65536, 64], P(('pix', 'peak')), may hold values from -0.8984375 to 0.8984375
- sec_factor: bfloat16 [8, 64], replicated, may hold values from -5 to 5
- peak_factor: bfloat16 [2048, 64], P('peak'), may hold values from -0.046875 to 0.046875
Outputs:
- grad_pix: float32 [65536, 64], P(('pix', 'peak'))
- grad_peak: float32 [2048, 64], P('peak')
The draws below stay inside these ranges and needn't reach their ends.
All inputs are finite; a program needn't handle non-finite values.
Results may differ from the reference program's by a relative error of at most 0.0003.
Values may be sent and summed in bfloat16 or wider, within the bound.
No kernel may reach another device: no remote copies, remote signals or barrier semaphores. Data moves between devices by JAX's collectives and lax.ppermute only.
A program may use at most 64 MiB of HBM per device.

```python
import math
import jax
import jax.numpy as jnp
from jax import lax

R = 64
PEAKS = 2048
S = 8
PIXELS = 65536


def shard_levels(own_key, dims, cuts, low, largest):
    def one(dim, shards_of):
        steps = jax.random.uniform(jax.random.fold_in(jax.random.fold_in(own_key, 6), dim), (shards_of,), jnp.float32, low / len(cuts), largest / len(cuts))
        return jnp.repeat(jnp.exp(steps), dims[dim] // shards_of).reshape((-1,) + (1,) * (len(dims) - dim - 1))

    gain = one(*cuts[0])
    for cut in cuts[1:]:
        gain = gain * one(*cut)
    return gain


def bell_draw(stream_key, dims, spread, bound, shards=(), kind=jnp.bfloat16):
    array = jax.random.normal(stream_key, dims, jnp.float32) * spread
    if len(shards) > 0:
        array = shard_levels(stream_key, dims, shards, -0.22, 0.18) * array
    return jnp.clip(array, min=-bound, max=bound).astype(kind)


def setup_inputs(seed: int = 0) -> dict:
    key_of = jax.random.split(jax.random.key(seed), 5)
    cube = bell_draw(key_of[0], (PIXELS, S, PEAKS), 1.0, 6.0, ((0, 16), (2, 16)))
    pix_factor = bell_draw(key_of[1], (PIXELS, R), 0.15, 0.8984375, ((0, 256),))
    sec_factor = bell_draw(key_of[2], (S, R), 1.0, 5.0)
    peak_factor = bell_draw(key_of[3], (PEAKS, R), (S * PEAKS) ** -0.5, 0.046875, ((0, 16),))
    return {"cube": cube, "pix_factor": pix_factor, "sec_factor": sec_factor, "peak_factor": peak_factor}


def reference(cube, pix_factor, sec_factor, peak_factor):
    fa = pix_factor.astype(jnp.float32)
    fb = sec_factor.astype(jnp.float32)
    fc = peak_factor.astype(jnp.float32)
    gram_a = jnp.dot(pix_factor.T, pix_factor, preferred_element_type=jnp.float32)
    gram_b = jnp.dot(sec_factor.T, sec_factor, preferred_element_type=jnp.float32)
    gram_c = jnp.dot(peak_factor.T, peak_factor, preferred_element_type=jnp.float32)
    pixels = cube.shape[0]
    sections = cube.shape[1]
    rank = peak_factor.shape[1]
    ttm = jnp.dot(cube.reshape(pixels * sections, cube.shape[2]), peak_factor, preferred_element_type=jnp.float32)
    ttm = ttm.reshape(pixels, sections, rank)
    mttkrp_pix = lax.optimization_barrier(jnp.sum(ttm * fb[None, :, :], axis=1))
    mttkrp_peak = jnp.zeros((cube.shape[2], rank), jnp.float32)
    for index in range(sections):
        inner = jnp.dot(cube[:, index, :].T, pix_factor, preferred_element_type=jnp.float32)
        mttkrp_peak = mttkrp_peak + inner * fb[index][None, :]
    grad_pix = mttkrp_pix - jnp.dot(fa, gram_b * gram_c, precision=lax.Precision.HIGHEST)
    scale = 1.0 / math.sqrt(float(sections * pixels))
    grad_peak = (mttkrp_peak - jnp.dot(fc, gram_a * gram_b, precision=lax.Precision.HIGHEST)) * scale
    return (grad_pix, grad_peak)
```

```python
import math

import jax
import jax.numpy as jnp
from jax import lax
from jax.experimental import pallas as pl
from jax.experimental.pallas import tpu as pltpu
from jax.sharding import Mesh
from jax.sharding import PartitionSpec as P

f32, bf16 = jnp.float32, jnp.bfloat16
NN = (((1,), (0,)), ((), ()))
NT = (((1,), (1,)), ((), ()))
PIX = ("xh", "z")
PEAK = ("y", "xl", "c")


def dot(a, b, dims=NN):
    return lax.dot_general(a, b, dims, preferred_element_type=f32)


def dot_split(w, b, dims=NN):
    hi = w.astype(bf16)
    rest = w - hi.astype(f32)
    mid = rest.astype(bf16)
    low = (rest - mid.astype(f32)).astype(bf16)
    return dot(hi, b, dims) + (dot(mid, b, dims) + dot(low, b, dims))


def both_modes(core, cube, own, other, ct_ref, b_ref, keep, send, peak, xbuf, wide, flat, wt, acc, sems):
    blocks, sections = xbuf.shape[0], b_ref.shape[0]
    pixels = xbuf.shape[1] // sections
    rank, peaks = ct_ref.shape
    mine = core[0]

    def copy(step):
        index = 2 * (step // 2) + lax.bitwise_xor(mine, step % 2)
        return pltpu.make_async_copy(cube.at[index], xbuf.at[step], sems.at[step])

    for step in range(blocks):
        copy(step).start()
    bt = jnp.transpose(b_ref[...].astype(f32))
    ct = ct_ref[...]
    for s in range(sections):
        product = ct.astype(f32) * bt[:, s : s + 1]
        hi = product.astype(bf16)
        wt[0:rank, s * peaks : (s + 1) * peaks] = hi
        wt[rank:, s * peaks : (s + 1) * peaks] = (product - hi.astype(f32)).astype(bf16)
    gram_b = dot(bt.astype(bf16), bt.astype(bf16), NT)
    weight = gram_b * dot(ct, ct, NT)
    gram_a = jnp.zeros((rank, rank), f32)
    acc[...] = jnp.zeros_like(acc)
    for step in range(blocks):
        at = own[step // 2] if step % 2 == 0 else other[step // 2]
        slot = step % 2
        gram_a = gram_a + dot(at, at, NT)
        copy(step).wait()
        wide[slot] = xbuf[step].astype(f32)
        for s in range(sections):
            rows = wide[slot, pl.ds(s, pixels, stride=sections), :]
            flat[slot, :, s * peaks : (s + 1) * peaks] = rows.astype(bf16)
        y = flat[slot]
        out = dot(wt[...], y, NT)
        out = out[0:rank] + out[rank:] - dot_split(weight, at)
        if step % 2 == 0:
            keep[step // 2] = out
        else:
            send[step // 2] = out
        acc[...] += dot(at, y)
    total = -dot_split(gram_a * gram_b, ct)
    for s in range(sections):
        total = total + acc[:, s * peaks : (s + 1) * peaks] * bt[:, s : s + 1]
    peak[...] = total


def call_both_modes(core, cube, own, other, ct, b):
    blocks, rows, peaks = cube.shape
    half, rank, pixels = own.shape
    vmem = pl.BlockSpec(memory_space=pltpu.VMEM)
    return pl.pallas_call(
        both_modes,
        out_shape=(
            jax.ShapeDtypeStruct((half, rank, pixels), f32),
            jax.ShapeDtypeStruct((half, rank, pixels), f32),
            jax.ShapeDtypeStruct((rank, peaks), f32),
        ),
        in_specs=[pl.BlockSpec(memory_space=pltpu.SMEM), pl.BlockSpec(memory_space=pltpu.HBM)] + [vmem] * 4,
        out_specs=(vmem, vmem, vmem),
        scratch_shapes=[
            pltpu.VMEM((blocks, rows, peaks), bf16),
            pltpu.VMEM((2, rows, peaks), f32),
            pltpu.VMEM((2, pixels, rows // pixels * peaks), bf16),
            pltpu.VMEM((2 * rank, rows // pixels * peaks), bf16),
            pltpu.VMEM((rank, rows // pixels * peaks), f32),
            pltpu.SemaphoreType.DMA((blocks,)),
        ],
        compiler_params=pltpu.CompilerParams(vmem_limit_bytes=40 << 20),
        cost_estimate=pl.CostEstimate(flops=3 * 10**9, bytes_accessed=10 << 20, transcendentals=0),
        name="both_modes",
    )(core, cube, own, other, ct, b)


def on_device(cube, pix_factor, sec_factor, peak_factor):
    pixels, sections, peaks = cube.shape
    rank = peak_factor.shape[1]
    core = lax.axis_index("c").astype(jnp.int32).reshape(1)
    swap = [(0, 1), (1, 0)]
    at = pix_factor.T
    ct = peak_factor.T
    own_pixels = at.shape[1]
    spread = jnp.broadcast_to(at[None], (8,) + at.shape)
    own = lax.all_to_all(spread, ("y", "xl"), 0, 0, tiled=True)
    other = lax.ppermute(own, "c", swap)
    cube = cube.reshape(pixels // own_pixels, own_pixels * sections, peaks)
    keep, send, part = call_both_modes(core, cube, own, other, ct, sec_factor)
    keep = keep + lax.ppermute(send, "c", swap)
    blocks = lax.all_to_all(keep, ("y", "xl"), 0, 0, tiled=True)
    grad_pix = jnp.sum(blocks, axis=0).T
    copies = jnp.broadcast_to(part[None], (16,) + part.shape)
    parts = lax.all_to_all(copies, PIX, 0, 0, tiled=True)
    scale = 1.0 / math.sqrt(float(sections * pixels * 16))
    grad_peak = (jnp.sum(parts, axis=0) * scale).T
    return (grad_pix, grad_peak)


def solution(mesh):
    split = Mesh(mesh.devices.reshape(2, 8, 4, 2, 2), PIX + PEAK)
    in_specs = (P(PIX, None, PEAK), P(PIX + PEAK, None), P(), P(PEAK, None))
    out_specs = (P(PIX + PEAK, None), P(PEAK, None))
    return jax.shard_map(
        on_device, mesh=split, in_specs=in_specs, out_specs=out_specs, check_vma=False
    )
```

```python
import math

import jax
import jax.numpy as jnp
from jax import lax
from jax.experimental import pallas as pl
from jax.experimental.pallas import tpu as pltpu
from jax.sharding import Mesh
from jax.sharding import PartitionSpec as P

f32, bf16 = jnp.float32, jnp.bfloat16
NN = (((1,), (0,)), ((), ()))
NT = (((1,), (1,)), ((), ()))
PIX = ("xh", "z")
PEAK = ("y", "xl", "c")
VMEM = pl.BlockSpec(memory_space=pltpu.VMEM)
ANY = pl.BlockSpec(memory_space=pl.ANY)
GRANT = 56 << 20


def dot(a, b, dims=NN):
    return lax.dot_general(a, b, dims, preferred_element_type=f32)


def dot_split(w, b, dims=NN):
    hi = w.astype(bf16)
    rest = w - hi.astype(f32)
    mid = rest.astype(bf16)
    low = (rest - mid.astype(f32)).astype(bf16)
    return dot(hi, b, dims) + (dot(mid, b, dims) + dot(low, b, dims))


def by_pixel(source, wide, sections):
    pixels = source.shape[0] // sections
    wide[...] = source[...].astype(f32)
    return jnp.concatenate(
        [wide[pl.ds(s, pixels, stride=sections), :].astype(bf16) for s in range(sections)], axis=1
    )


def stream(cube, xbuf, sems, ahead, body):
    pairs = xbuf.shape[0]

    def copy(pair):
        return pltpu.make_async_copy(cube.at[pl.ds(2 * pair, 2)], xbuf.at[pair], sems.at[pair])

    for pair in range(ahead):
        copy(pair).start()
    yield
    for pair in range(pairs):
        if pair + ahead < pairs:
            copy(pair + ahead).start()
        copy(pair).wait()
        body(pair)
    yield


def pixel_mode(cube, ct_hbm, b_hbm, out, ct_ref, b_ref, xbuf, wide, wt, obuf, insems, sems, outsems):
    sections = b_ref.shape[0]
    rank, peaks = ct_ref.shape
    small = [
        pltpu.make_async_copy(ct_hbm, ct_ref, insems.at[0]),
        pltpu.make_async_copy(b_hbm, b_ref, insems.at[1]),
    ]
    for each in small:
        each.start()

    def copy_out(pair):
        two = pl.ds(2 * pair, 2)
        return pltpu.make_async_copy(obuf.at[two], out.at[two], outsems.at[pair])

    def body(pair):
        for part in range(2):
            y = by_pixel(xbuf.at[pair, part], wide.at[part], sections)
            both = jnp.transpose(dot(y, wt[...]))
            obuf[2 * pair + part, 0:rank] = both[0:rank] + both[rank:]
            obuf[2 * pair + part, rank:] = gram
        copy_out(pair).start()

    run = stream(cube, xbuf, sems, 2, body)
    next(run)
    for each in small:
        each.wait()
    bt = jnp.transpose(b_ref[...].astype(f32))
    ct = ct_ref[...]
    gram = dot(ct, ct, NT)
    quarter = rank // 4
    gram = jnp.concatenate([gram[i * quarter : (i + 1) * quarter] for i in range(4)], axis=1)
    for s in range(sections):
        product = ct.astype(f32) * bt[:, s : s + 1]
        hi = product.astype(bf16).astype(f32)
        both = jnp.concatenate([hi, product - hi], axis=0)
        wt[s * peaks : (s + 1) * peaks, :] = jnp.transpose(both).astype(bf16)
    next(run)
    for pair in range(xbuf.shape[0]):
        copy_out(pair).wait()


def call_pixel_mode(cube, ct, b):
    blocks, rows, peaks = cube.shape
    rank = ct.shape[0]
    sections = b.shape[0]
    part = (blocks, rank + rank // 4, rows // sections)
    return pl.pallas_call(
        pixel_mode,
        out_shape=jax.ShapeDtypeStruct(part, f32),
        in_specs=[ANY, ANY, ANY],
        out_specs=ANY,
        scratch_shapes=[
            pltpu.VMEM(ct.shape, bf16),
            pltpu.VMEM(b.shape, bf16),
            pltpu.VMEM((blocks // 2, 2, rows, peaks), bf16),
            pltpu.VMEM((2, rows, peaks), f32),
            pltpu.VMEM((sections * peaks, 2 * rank), bf16),
            pltpu.VMEM(part, f32),
            pltpu.SemaphoreType.DMA((2,)),
            pltpu.SemaphoreType.DMA((blocks // 2,)),
            pltpu.SemaphoreType.DMA((blocks // 2,)),
        ],
        compiler_params=pltpu.CompilerParams(vmem_limit_bytes=GRANT),
        cost_estimate=pl.CostEstimate(flops=2 * 10**9, bytes_accessed=20 << 20, transcendentals=0),
        name="pixel_mode",
    )(cube, ct, b)


def peak_mode(cube, rows_hbm, ct_hbm, b_hbm, peak, rows, ct_ref, b_ref, xbuf, wide, acc, insems, sems):
    sections, rank = b_ref.shape
    peaks = peak.shape[1]
    small = [
        pltpu.make_async_copy(rows_hbm, rows, insems.at[0]),
        pltpu.make_async_copy(ct_hbm, ct_ref, insems.at[1]),
        pltpu.make_async_copy(b_hbm, b_ref, insems.at[2]),
    ]
    for each in small:
        each.start()

    def body(pair):
        total = None
        for part in range(2):
            y = by_pixel(xbuf.at[pair, part], wide.at[2 * (pair % 2) + part], sections)
            term = dot(rows[2 * pair + part], y)
            total = term if total is None else total + term
        acc[...] += total

    run = stream(cube, xbuf, sems, 3, body)
    next(run)
    for each in small:
        each.wait()
    bt = jnp.transpose(b_ref[...].astype(f32))
    gram_a = jnp.zeros((rank, rank), f32)
    for index in range(rows.shape[0]):
        gram_a = gram_a + dot(rows[index], rows[index], NT)
    gram_b = dot(bt.astype(bf16), bt.astype(bf16), NT)
    total = -dot_split(gram_a * gram_b, ct_ref[...])
    acc[...] = jnp.zeros_like(acc)
    next(run)
    for s in range(sections):
        total = total + acc[:, s * peaks : (s + 1) * peaks] * bt[:, s : s + 1]
    peak[...] = total


def call_peak_mode(cube, own, ct, b):
    blocks, rows, peaks = cube.shape
    rank = ct.shape[0]
    return pl.pallas_call(
        peak_mode,
        out_shape=jax.ShapeDtypeStruct((rank, peaks), f32),
        in_specs=[ANY, ANY, ANY, ANY],
        out_specs=VMEM,
        scratch_shapes=[
            pltpu.VMEM(own.shape, bf16),
            pltpu.VMEM(ct.shape, bf16),
            pltpu.VMEM(b.shape, bf16),
            pltpu.VMEM((blocks // 2, 2, rows, peaks), bf16),
            pltpu.VMEM((4, rows, peaks), f32),
            pltpu.VMEM((rank, b.shape[0] * peaks), f32),
            pltpu.SemaphoreType.DMA((3,)),
            pltpu.SemaphoreType.DMA((blocks // 2,)),
        ],
        compiler_params=pltpu.CompilerParams(vmem_limit_bytes=GRANT),
        cost_estimate=pl.CostEstimate(flops=10**9, bytes_accessed=10 << 20, transcendentals=0),
        name="peak_mode",
    )(cube, own, ct, b)


def finish_pixels(blocks, at_ref, b_ref, out):
    rank = out.shape[0]
    total = blocks[0]
    for index in range(1, blocks.shape[0]):
        total = total + blocks[index]
    gram = total[rank:]
    gram_c = jnp.concatenate([gram[:, i * rank : (i + 1) * rank] for i in range(4)], axis=0)
    bt = jnp.transpose(b_ref[...].astype(f32)).astype(bf16)
    out[...] = total[0:rank] - dot_split(dot(bt, bt, NT) * gram_c, at_ref[...])


def call_finish_pixels(blocks, at, b):
    return pl.pallas_call(
        finish_pixels,
        out_shape=jax.ShapeDtypeStruct(at.shape, f32),
        in_specs=[VMEM] * 3,
        out_specs=VMEM,
        cost_estimate=pl.CostEstimate(flops=10**7, bytes_accessed=1 << 20, transcendentals=0),
        name="finish_pixels",
    )(blocks, at, b)


def on_device(cube, pix_factor, sec_factor, peak_factor):
    pixels, sections, peaks = cube.shape
    at = pix_factor.T
    ct = peak_factor.T
    cube = cube.reshape(pixels // at.shape[1], at.shape[1] * sections, peaks)
    own = lax.all_to_all(jnp.broadcast_to(at[None], (16,) + at.shape), PEAK, 0, 0, tiled=True)
    sums = call_pixel_mode(cube, ct, sec_factor)
    sums, own = lax.optimization_barrier((sums, own))
    part = call_peak_mode(cube, own, ct, sec_factor)
    sums, part = lax.optimization_barrier((sums, part))
    blocks = lax.all_to_all(sums, PEAK, 0, 0, tiled=True)
    for axis, step in (("z", 1), ("z", 2), ("z", 4)):
        pairs = [(i, i ^ step) for i in range(lax.axis_size(axis))]
        part = part + lax.ppermute(part, axis, pairs)
    other = lax.ppermute(part, "xh", [(0, 1), (1, 0)])
    grad_pix = call_finish_pixels(blocks, at, sec_factor).T
    other, grad_pix = lax.optimization_barrier((other, grad_pix))
    part = part + other
    scale = 1.0 / math.sqrt(float(sections * pixels * 16))
    grad_peak = (part * scale).T
    return (grad_pix, grad_peak)


def solution(mesh):
    split = Mesh(mesh.devices.reshape(2, 8, 4, 2, 2), PIX + PEAK)
    in_specs = (P(PIX, None, PEAK), P(PIX + PEAK, None), P(), P(PEAK, None))
    out_specs = (P(PIX + PEAK, None), P(PEAK, None))
    return jax.shard_map(
        on_device, mesh=split, in_specs=in_specs, out_specs=out_specs, check_vma=False
    )
```

```python
import math

import jax
import jax.numpy as jnp
from jax import lax
from jax.experimental import pallas as pl
from jax.experimental.pallas import tpu as pltpu
from jax.sharding import Mesh
from jax.sharding import PartitionSpec as P

f32, bf16 = jnp.float32, jnp.bfloat16
NN = (((1,), (0,)), ((), ()))
NT = (((1,), (1,)), ((), ()))
PIX = ("xh", "z")
PEAK = ("y", "xl", "c")
VMEM = pl.BlockSpec(memory_space=pltpu.VMEM)
ANY = pl.BlockSpec(memory_space=pl.ANY)
GRANT = 56 << 20


def dot(a, b, dims=NN):
    return lax.dot_general(a, b, dims, preferred_element_type=f32)


def dot_split(w, b, dims=NN):
    hi = w.astype(bf16)
    rest = w - hi.astype(f32)
    mid = rest.astype(bf16)
    low = (rest - mid.astype(f32)).astype(bf16)
    return dot(hi, b, dims) + (dot(mid, b, dims) + dot(low, b, dims))


def by_pixel(source, wide, sections):
    pixels = source.shape[0] // sections
    wide[...] = source[...].astype(f32)
    return jnp.concatenate(
        [wide[pl.ds(s, pixels, stride=sections), :].astype(bf16) for s in range(sections)], axis=1
    )


def stream(cube, xbuf, sems, ahead, body):
    pairs = xbuf.shape[0]

    def copy(pair):
        return pltpu.make_async_copy(cube.at[pl.ds(2 * pair, 2)], xbuf.at[pair], sems.at[pair])

    for pair in range(ahead):
        copy(pair).start()
    yield
    for pair in range(pairs):
        if pair + ahead < pairs:
            copy(pair + ahead).start()
        copy(pair).wait()
        body(pair)
    yield


def pixel_mode(core, cube, ct_hbm, b_hbm, keep, send, ct_ref, b_ref, xbuf, wide, wt, obuf, insems, sems, outsems):
    sections = b_ref.shape[0]
    rank, peaks = ct_ref.shape
    small = [
        pltpu.make_async_copy(ct_hbm, ct_ref, insems.at[0]),
        pltpu.make_async_copy(b_hbm, b_ref, insems.at[1]),
    ]
    for each in small:
        each.start()

    def copy_out(pair):
        return [
            pltpu.make_async_copy(obuf.at[part, pair], out.at[pair], outsems.at[part, pair])
            for part, out in enumerate((keep, send))
        ]

    def body(pair):
        for part in range(2):
            y = by_pixel(xbuf.at[pair, lax.bitwise_xor(core[0], part)], wide.at[part], sections)
            both = jnp.transpose(dot(y, wt[...]))
            obuf[part, pair, 0:rank] = both[0:rank] + both[rank:]
            obuf[part, pair, rank:] = gram
        for each in copy_out(pair):
            each.start()

    run = stream(cube, xbuf, sems, 2, body)
    next(run)
    for each in small:
        each.wait()
    bt = jnp.transpose(b_ref[...].astype(f32))
    ct = ct_ref[...]
    gram = dot(ct, ct, NT)
    quarter = rank // 4
    gram = jnp.concatenate([gram[i * quarter : (i + 1) * quarter] for i in range(4)], axis=1)
    for s in range(sections):
        product = ct.astype(f32) * bt[:, s : s + 1]
        hi = product.astype(bf16).astype(f32)
        both = jnp.concatenate([hi, product - hi], axis=0)
        wt[s * peaks : (s + 1) * peaks, :] = jnp.transpose(both).astype(bf16)
    next(run)
    for pair in range(xbuf.shape[0]):
        for each in copy_out(pair):
            each.wait()


def call_pixel_mode(core, cube, ct, b):
    blocks, rows, peaks = cube.shape
    rank = ct.shape[0]
    sections = b.shape[0]
    part = (blocks // 2, rank + rank // 4, rows // sections)
    return pl.pallas_call(
        pixel_mode,
        out_shape=(jax.ShapeDtypeStruct(part, f32),) * 2,
        in_specs=[pl.BlockSpec(memory_space=pltpu.SMEM), ANY, ANY, ANY],
        out_specs=(ANY, ANY),
        scratch_shapes=[
            pltpu.VMEM(ct.shape, bf16),
            pltpu.VMEM(b.shape, bf16),
            pltpu.VMEM((blocks // 2, 2, rows, peaks), bf16),
            pltpu.VMEM((2, rows, peaks), f32),
            pltpu.VMEM((sections * peaks, 2 * rank), bf16),
            pltpu.VMEM((2,) + part, f32),
            pltpu.SemaphoreType.DMA((2,)),
            pltpu.SemaphoreType.DMA((blocks // 2,)),
            pltpu.SemaphoreType.DMA((2, blocks // 2)),
        ],
        compiler_params=pltpu.CompilerParams(vmem_limit_bytes=GRANT),
        cost_estimate=pl.CostEstimate(flops=2 * 10**9, bytes_accessed=20 << 20, transcendentals=0),
        name="pixel_mode",
    )(core, cube, ct, b)


def peak_mode(cube, rows_hbm, ct_hbm, b_hbm, peak, rows, ct_ref, b_ref, xbuf, wide, acc, gram, insems, sems):
    sections, rank = b_ref.shape
    peaks = peak.shape[1]
    small = [
        pltpu.make_async_copy(rows_hbm, rows, insems.at[0]),
        pltpu.make_async_copy(ct_hbm, ct_ref, insems.at[1]),
        pltpu.make_async_copy(b_hbm, b_ref, insems.at[2]),
    ]
    for each in small:
        each.start()

    def body(pair):
        total, squares = acc[...], gram[...]
        for part in range(2):
            at = rows[2 * pair + part]
            y = by_pixel(xbuf.at[pair, part], wide.at[2 * (pair % 2) + part], sections)
            total = total + dot(at, y)
            squares = squares + dot(at, at, NT)
        acc[...] = total
        gram[...] = squares

    run = stream(cube, xbuf, sems, 3, body)
    next(run)
    acc[...] = jnp.zeros_like(acc)
    gram[...] = jnp.zeros_like(gram)
    for each in small:
        each.wait()
    bt = jnp.transpose(b_ref[...].astype(f32))
    gram_b = dot(bt.astype(bf16), bt.astype(bf16), NT)
    next(run)
    total = -dot_split(gram[...] * gram_b, ct_ref[...])
    for s in range(sections):
        total = total + acc[:, s * peaks : (s + 1) * peaks] * bt[:, s : s + 1]
    peak[...] = total


def call_peak_mode(cube, own, ct, b):
    blocks, rows, peaks = cube.shape
    rank = ct.shape[0]
    return pl.pallas_call(
        peak_mode,
        out_shape=jax.ShapeDtypeStruct((rank, peaks), f32),
        in_specs=[ANY, ANY, ANY, ANY],
        out_specs=VMEM,
        scratch_shapes=[
            pltpu.VMEM(own.shape, bf16),
            pltpu.VMEM(ct.shape, bf16),
            pltpu.VMEM(b.shape, bf16),
            pltpu.VMEM((blocks // 2, 2, rows, peaks), bf16),
            pltpu.VMEM((4, rows, peaks), f32),
            pltpu.VMEM((rank, b.shape[0] * peaks), f32),
            pltpu.VMEM((rank, rank), f32),
            pltpu.SemaphoreType.DMA((3,)),
            pltpu.SemaphoreType.DMA((blocks // 2,)),
        ],
        compiler_params=pltpu.CompilerParams(vmem_limit_bytes=52 << 20),
        cost_estimate=pl.CostEstimate(flops=10**9, bytes_accessed=10 << 20, transcendentals=0),
        name="peak_mode",
    )(cube, own, ct, b)


def finish_pixels(blocks, at_ref, b_ref, out):
    rank = out.shape[0]
    total = blocks[0]
    for index in range(1, blocks.shape[0]):
        total = total + blocks[index]
    gram = total[rank:]
    gram_c = jnp.concatenate([gram[:, i * rank : (i + 1) * rank] for i in range(4)], axis=0)
    bt = jnp.transpose(b_ref[...].astype(f32)).astype(bf16)
    out[...] = total[0:rank] - dot_split(dot(bt, bt, NT) * gram_c, at_ref[...])


def call_finish_pixels(blocks, at, b):
    return pl.pallas_call(
        finish_pixels,
        out_shape=jax.ShapeDtypeStruct(at.shape, f32),
        in_specs=[VMEM] * 3,
        out_specs=VMEM,
        compiler_params=pltpu.CompilerParams(vmem_limit_bytes=8 << 20),
        cost_estimate=pl.CostEstimate(flops=10**7, bytes_accessed=1 << 20, transcendentals=0),
        name="finish_pixels",
    )(blocks, at, b)


def add(a_ref, b_ref, out):
    out[...] = a_ref[...] + b_ref[...]


def call_add(a, b):
    return pl.pallas_call(
        add,
        out_shape=jax.ShapeDtypeStruct(a.shape, f32),
        in_specs=[VMEM] * 2,
        out_specs=VMEM,
        compiler_params=pltpu.CompilerParams(vmem_limit_bytes=1 << 20),
        cost_estimate=pl.CostEstimate(flops=2000000000, bytes_accessed=2000000000 // 300, transcendentals=0),
        name="add",
    )(a, b)


def exchange(value, axis, step):
    return lax.ppermute(value, axis, [(i, i ^ step) for i in range(lax.axis_size(axis))])


def on_device(cube, pix_factor, sec_factor, peak_factor):
    pixels, sections, peaks = cube.shape
    at = pix_factor.T
    ct = peak_factor.T
    cube = cube.reshape(pixels // at.shape[1], at.shape[1] * sections, peaks)
    own = lax.all_to_all(jnp.broadcast_to(at[None], (16,) + at.shape), PEAK, 0, 0, tiled=True)
    core = lax.axis_index("c").astype(jnp.int32).reshape(1)
    keep, send = call_pixel_mode(core, cube, ct, sec_factor)
    send, own = lax.optimization_barrier((send, own))
    received = exchange(send, "c", 1)
    part = call_peak_mode(cube, own, ct, sec_factor)
    received, part = lax.optimization_barrier((received, part))
    blocks = lax.all_to_all(keep + received, ("y", "xl"), 0, 0, tiled=True)
    for step in (4, 2, 1):
        part = call_add(part, exchange(part, "z", step))
    other = exchange(part, "xh", 1)
    grad_pix = call_finish_pixels(blocks, at, sec_factor).T
    other, grad_pix = lax.optimization_barrier((other, grad_pix))
    scale = 1.0 / math.sqrt(float(sections * pixels * 16))
    grad_peak = ((part + other) * scale).T
    return (grad_pix, grad_peak)


def solution(mesh):
    split = Mesh(mesh.devices.reshape(2, 8, 4, 2, 2), PIX + PEAK)
    in_specs = (P(PIX, None, PEAK), P(PIX + PEAK, None), P(), P(PEAK, None))
    out_specs = (P(PIX + PEAK, None), P(PEAK, None))
    return jax.shard_map(
        on_device, mesh=split, in_specs=in_specs, out_specs=out_specs, check_vma=False
    )
```

```python
import math

import jax
import jax.numpy as jnp
from jax import lax
from jax.experimental import pallas as pl
from jax.experimental.pallas import tpu as pltpu
from jax.sharding import Mesh
from jax.sharding import PartitionSpec as P

f32, bf16 = jnp.float32, jnp.bfloat16
NN = (((1,), (0,)), ((), ()))
NT = (((1,), (1,)), ((), ()))
PIX = ("xh", "z")
PEAK = ("y", "xl", "c")
VMEM = pl.BlockSpec(memory_space=pltpu.VMEM)
ANY = pl.BlockSpec(memory_space=pl.ANY)
GRANT = 56 << 20


def dot(a, b, dims=NN):
    return lax.dot_general(a, b, dims, preferred_element_type=f32)


def dot_split(w, b, dims=NN):
    hi = w.astype(bf16)
    rest = w - hi.astype(f32)
    mid = rest.astype(bf16)
    low = (rest - mid.astype(f32)).astype(bf16)
    return dot(hi, b, dims) + (dot(mid, b, dims) + dot(low, b, dims))


def by_pixel(source, wide, sections):
    pixels = source.shape[0] // sections
    wide[...] = source[...].astype(f32)
    return jnp.concatenate(
        [wide[pl.ds(s, pixels, stride=sections), :].astype(bf16) for s in range(sections)], axis=1
    )


def stream(cube, xbuf, sems, ahead, body):
    pairs = xbuf.shape[0]

    def copy(pair):
        return pltpu.make_async_copy(cube.at[pl.ds(2 * pair, 2)], xbuf.at[pair], sems.at[pair])

    for pair in range(ahead):
        copy(pair).start()
    yield
    for pair in range(pairs):
        if pair + ahead < pairs:
            copy(pair + ahead).start()
        copy(pair).wait()
        body(pair)
    yield


def pixel_mode(core, cube, ct_hbm, b_hbm, keep, send, ct_ref, b_ref, xbuf, wide, wt, obuf, insems, sems, outsems):
    sections = b_ref.shape[0]
    rank, peaks = ct_ref.shape
    small = [
        pltpu.make_async_copy(ct_hbm, ct_ref, insems.at[0]),
        pltpu.make_async_copy(b_hbm, b_ref, insems.at[1]),
    ]
    for each in small:
        each.start()

    def copy_out(pair):
        return [
            pltpu.make_async_copy(obuf.at[part, pair], out.at[pair], outsems.at[part, pair])
            for part, out in enumerate((keep, send))
        ]

    def body(pair):
        for part in range(2):
            y = by_pixel(xbuf.at[pair, lax.bitwise_xor(core[0], part)], wide.at[part], sections)
            both = jnp.transpose(dot(y, wt[...]))
            obuf[part, pair, 0:rank] = both[0:rank] + both[rank:]
            obuf[part, pair, rank:] = gram
        for each in copy_out(pair):
            each.start()

    run = stream(cube, xbuf, sems, 2, body)
    next(run)
    for each in small:
        each.wait()
    bt = jnp.transpose(b_ref[...].astype(f32))
    ct = ct_ref[...]
    gram = dot(ct, ct, NT)
    quarter = rank // 4
    gram = jnp.concatenate([gram[i * quarter : (i + 1) * quarter] for i in range(4)], axis=1)
    for s in range(sections):
        product = ct.astype(f32) * bt[:, s : s + 1]
        hi = product.astype(bf16).astype(f32)
        both = jnp.concatenate([hi, product - hi], axis=0)
        wt[s * peaks : (s + 1) * peaks, :] = jnp.transpose(both).astype(bf16)
    next(run)
    for pair in range(xbuf.shape[0]):
        for each in copy_out(pair):
            each.wait()


def call_pixel_mode(core, cube, ct, b):
    blocks, rows, peaks = cube.shape
    rank = ct.shape[0]
    sections = b.shape[0]
    part = (blocks // 2, rank + rank // 4, rows // sections)
    return pl.pallas_call(
        pixel_mode,
        out_shape=(jax.ShapeDtypeStruct(part, f32),) * 2,
        in_specs=[pl.BlockSpec(memory_space=pltpu.SMEM), ANY, ANY, ANY],
        out_specs=(ANY, ANY),
        scratch_shapes=[
            pltpu.VMEM(ct.shape, bf16),
            pltpu.VMEM(b.shape, bf16),
            pltpu.VMEM((blocks // 2, 2, rows, peaks), bf16),
            pltpu.VMEM((2, rows, peaks), f32),
            pltpu.VMEM((sections * peaks, 2 * rank), bf16),
            pltpu.VMEM((2,) + part, f32),
            pltpu.SemaphoreType.DMA((2,)),
            pltpu.SemaphoreType.DMA((blocks // 2,)),
            pltpu.SemaphoreType.DMA((2, blocks // 2)),
        ],
        compiler_params=pltpu.CompilerParams(vmem_limit_bytes=GRANT),
        cost_estimate=pl.CostEstimate(flops=2 * 10**9, bytes_accessed=20 << 20, transcendentals=0),
        name="pixel_mode",
    )(core, cube, ct, b)


def peak_mode(cube, rows_hbm, ct_hbm, b_hbm, peak, rows, ct_ref, b_ref, xbuf, wide, acc, gram, insems, sems):
    sections, rank = b_ref.shape
    peaks = peak.shape[1]
    small = [
        pltpu.make_async_copy(rows_hbm, rows, insems.at[0]),
        pltpu.make_async_copy(ct_hbm, ct_ref, insems.at[1]),
        pltpu.make_async_copy(b_hbm, b_ref, insems.at[2]),
    ]
    for each in small:
        each.start()

    def body(pair):
        total, squares = acc[...], gram[...]
        for part in range(2):
            at = rows[2 * pair + part]
            y = by_pixel(xbuf.at[pair, part], wide.at[2 * (pair % 2) + part], sections)
            total = total + dot(at, y)
            squares = squares + dot(at, at, NT)
        acc[...] = total
        gram[...] = squares

    run = stream(cube, xbuf, sems, 3, body)
    next(run)
    acc[...] = jnp.zeros_like(acc)
    gram[...] = jnp.zeros_like(gram)
    for each in small:
        each.wait()
    bt = jnp.transpose(b_ref[...].astype(f32))
    gram_b = dot(bt.astype(bf16), bt.astype(bf16), NT)
    next(run)
    total = -dot_split(gram[...] * gram_b, ct_ref[...])
    for s in range(sections):
        total = total + acc[:, s * peaks : (s + 1) * peaks] * bt[:, s : s + 1]
    peak[...] = total


def call_peak_mode(cube, own, ct, b):
    blocks, rows, peaks = cube.shape
    rank = ct.shape[0]
    return pl.pallas_call(
        peak_mode,
        out_shape=jax.ShapeDtypeStruct((rank, peaks), f32),
        in_specs=[ANY, ANY, ANY, ANY],
        out_specs=VMEM,
        scratch_shapes=[
            pltpu.VMEM(own.shape, bf16),
            pltpu.VMEM(ct.shape, bf16),
            pltpu.VMEM(b.shape, bf16),
            pltpu.VMEM((blocks // 2, 2, rows, peaks), bf16),
            pltpu.VMEM((4, rows, peaks), f32),
            pltpu.VMEM((rank, b.shape[0] * peaks), f32),
            pltpu.VMEM((rank, rank), f32),
            pltpu.SemaphoreType.DMA((3,)),
            pltpu.SemaphoreType.DMA((blocks // 2,)),
        ],
        compiler_params=pltpu.CompilerParams(vmem_limit_bytes=52 << 20),
        cost_estimate=pl.CostEstimate(flops=10**9, bytes_accessed=10 << 20, transcendentals=0),
        name="peak_mode",
    )(cube, own, ct, b)


def finish_pixels(blocks, at_ref, b_ref, out):
    rank = out.shape[0]
    total = blocks[0]
    for index in range(1, blocks.shape[0]):
        total = total + blocks[index]
    gram = total[rank:]
    gram_c = jnp.concatenate([gram[:, i * rank : (i + 1) * rank] for i in range(4)], axis=0)
    bt = jnp.transpose(b_ref[...].astype(f32)).astype(bf16)
    out[...] = total[0:rank] - dot_split(dot(bt, bt, NT) * gram_c, at_ref[...])


def call_finish_pixels(blocks, at, b):
    return pl.pallas_call(
        finish_pixels,
        out_shape=jax.ShapeDtypeStruct(at.shape, f32),
        in_specs=[VMEM] * 3,
        out_specs=VMEM,
        compiler_params=pltpu.CompilerParams(vmem_limit_bytes=8 << 20),
        cost_estimate=pl.CostEstimate(flops=10**7, bytes_accessed=1 << 20, transcendentals=0),
        name="finish_pixels",
    )(blocks, at, b)


def add(a_ref, b_ref, out):
    out[...] = a_ref[...] + b_ref[...]


def call_add(a, b):
    return pl.pallas_call(
        add,
        out_shape=jax.ShapeDtypeStruct(a.shape, f32),
        in_specs=[VMEM] * 2,
        out_specs=VMEM,
        compiler_params=pltpu.CompilerParams(vmem_limit_bytes=1 << 20),
        cost_estimate=pl.CostEstimate(flops=2000000000, bytes_accessed=2000000000 // 300, transcendentals=0),
        name="add",
    )(a, b)


def exchange(value, axis, step):
    return lax.ppermute(value, axis, [(i, i ^ step) for i in range(lax.axis_size(axis))])


def on_device(cube, pix_factor, sec_factor, peak_factor):
    pixels, sections, peaks = cube.shape
    at = pix_factor.T
    ct = peak_factor.T
    cube = cube.reshape(pixels // at.shape[1], at.shape[1] * sections, peaks)
    own = lax.all_to_all(jnp.broadcast_to(at[None], (16,) + at.shape), PEAK, 0, 0, tiled=True)
    core = lax.axis_index("c").astype(jnp.int32).reshape(1)
    keep, send = call_pixel_mode(core, cube, ct, sec_factor)
    send, own = lax.optimization_barrier((send, own))
    received = exchange(send, "c", 1)
    part = call_peak_mode(cube, own, ct, sec_factor)
    received, part = lax.optimization_barrier((received, part))
    blocks = lax.all_to_all(keep + received, ("y", "xl"), 0, 0, tiled=True)
    part = call_add(part, exchange(part, "xh", 1))
    for step in (6, 2):
        part = call_add(part, exchange(part, "z", step))
    other = exchange(part, "z", 1)
    grad_pix = call_finish_pixels(blocks, at, sec_factor).T
    other, grad_pix = lax.optimization_barrier((other, grad_pix))
    scale = 1.0 / math.sqrt(float(sections * pixels * 16))
    grad_peak = ((part + other) * scale).T
    return (grad_pix, grad_peak)


def solution(mesh):
    split = Mesh(mesh.devices.reshape(2, 8, 4, 2, 2), PIX + PEAK)
    in_specs = (P(PIX, None, PEAK), P(PIX + PEAK, None), P(), P(PEAK, None))
    out_specs = (P(PIX + PEAK, None), P(PEAK, None))
    return jax.shard_map(
        on_device, mesh=split, in_specs=in_specs, out_specs=out_specs, check_vma=False
    )
```
